32 devices in a mesh: grp: 2 (over x), ctx: 16 (over z, y, core).
Axes of the slice: x: 2, y: 2, z: 4, core: 2. Of those that a mesh axis runs over, the one named last changes fastest.
Arguments:
- queries: bfloat16 [4096, 4096], P(('grp', 'ctx')), parts along dimension 0, may hold values from -6 to 6
- keys_values: bfloat16 [4096, 2048], P(('grp', 'ctx')), parts along dimension 0, may hold values from -6 to 6
- depth_kernel: float32 [8, 2048], replicated, may hold values from -2.1 to 2.1
- point_weight: bfloat16 [2, 1024, 1024], replicated, may hold values from -0.1875 to 0.1875
- page_table: int32 [64], P('grp'), parts along dimension 0, may hold values from 0 to 31, each once
- doc_lengths: int32 [8], P('grp'), parts along dimension 0, may hold values from 1 to 1024, 2048 in all
Outputs:
- attended: bfloat16 [4096, 4096], P(('grp', 'ctx')), parts along dimension 0
- kv_tier: bfloat16 [1024, 2048], P(('grp', 'ctx')), parts along dimension 0
The draws below stay inside these ranges and needn't reach their ends.
There are 2 independent parts, one for each index of `grp`. The reference program is written for one: setup_inputs(seed, part) draws one part's arguments, and reference() takes and returns one part's arrays. A program takes and returns all parts, laid end to end along the dimension named above; an argument that names none is the same for every part. Nothing has to cross between parts.
Inputs may be any that keep to these rules, and one draw needn't show every extreme that they name: Slot s, the s-th page of the shards of queries and keys_values, holds logical page page_table[s]; every page stands in exactly one slot. `doc_lengths`: the documents lie end to end and cover the sequence.
All inputs are finite; a program needn't handle non-finite values.
Results may differ from the reference program's by a relative error of at most 0.0061.
Values may be sent and summed in bfloat16 or wider, within the bound.
A program may use at most 64 MiB of HBM per device.

```python
import math
import jax
import jax.numpy as jnp
import numpy as np
from jax import lax

KVH = 8
HD = 128
QH = 32
KERNEL = 8
STRIDE = 4
PAGE = 64
SPANS = 4
GROUP = 4
KV = 1024
CR_PAGE = 16
PAGES = 32
TOKENS = 2048
CROWS = 512


def levels(own_key, shape, split, low, top_value):
    loudness, own = 1.0, jax.random.fold_in(own_key, 6)
    for dim, parts in split:
        heights = jnp.exp(jax.random.uniform(jax.random.fold_in(own, dim), (parts,), jnp.float32, low / len(split), top_value / len(split)))
        loudness = loudness * jnp.repeat(heights, shape[dim] // parts).reshape([-1 if axis == dim else 1 for axis in range(len(shape))])
    return loudness


def length_profile(count, total, reach, skew):
    weights = [(1 << 20) // math.isqrt(grade ** skew) + 1 for grade in range(2, count + 1)]
    surplus, given = total - reach - (count - 1), [1] * (count - 1)
    while surplus > 0:
        candidates = [i for i in range(count - 1) if given[i] < reach]
        mass, remaining = sum([weights[i] for i in candidates]), surplus
        for i in candidates:
            more = min(reach - given[i], max(1, remaining * weights[i] // mass), surplus)
            given[i] = given[i] + more
            surplus = surplus - more
    return np.array([reach] + given)


def uneven_parts(key, number_of, total, most, skew):
    if number_of == 2:
        one = jax.random.randint(key, (), max(1, total - most), min(most, total - 1) + 1)
        return jnp.stack([one, total - one])
    tallies = jnp.asarray(length_profile(number_of, total, most, skew), jnp.int32)
    couples = (number_of - 1) // 2
    giver, receiver = tallies[1:1 + 2 * couples:2], tallies[2:2 + 2 * couples:2]
    slack = jnp.minimum(giver - 1, most - receiver)
    moved = jax.random.randint(jax.random.fold_in(key, 1), (couples,), 0, 1 << 20) % (slack + 1)
    tallies = tallies.at[1:1 + 2 * couples:2].set(giver - moved).at[2:2 + 2 * couples:2].set(receiver + moved)
    return tallies[jax.random.permutation(jax.random.fold_in(key, 2), number_of)]


def scatter_about(stream_key, dims, spread, reach, cuts=(), held_as=jnp.bfloat16):
    gain = levels(stream_key, dims, cuts, -0.22, 0.18) if cuts else 1.0
    values = jax.random.normal(stream_key, dims, jnp.float32) * spread * gain
    return jnp.minimum(jnp.maximum(values, -reach), reach).astype(held_as)


def setup_inputs(seed: int = 0, part: int = 0) -> dict:
    key_list = jax.random.split(jax.random.key(seed), 7)
    part_splits = jax.random.split(jax.random.fold_in(key_list[6], part), 7)
    return {
        "queries": scatter_about(part_splits[0], (TOKENS, QH * HD), 1.0, 6.0, ((0, 16),)),
        "keys_values": scatter_about(part_splits[1], (TOKENS, 2 * KV), 1.0, 6.0, ((0, 16),)),
        "depth_kernel": scatter_about(key_list[2], (KERNEL, 2 * KV), 0.35, 2.1, (), jnp.float32),
        "point_weight": scatter_about(key_list[3], (2, KV, KV), KV ** -0.5, 0.1875),
        "page_table": jax.random.permutation(part_splits[4], PAGES).astype(jnp.int32),
        "doc_lengths": uneven_parts(part_splits[5], SPANS, TOKENS, TOKENS // 2, 2).astype(jnp.int32),
    }


SCORE_SCALE = 6.0

def unit_rows(block, head_count):
    row_count = block.shape[0]
    pieces = block.astype(jnp.float32).reshape(row_count, head_count, -1)
    factor = lax.rsqrt(lax.optimization_barrier(jnp.mean(pieces * pieces, axis=2, keepdims=True)) + 1e-06)
    return (pieces * factor).astype(jnp.bfloat16)

def reference(queries, keys_values, depth_kernel, point_weight, page_table, doc_lengths):
    kv_width = KVH * HD
    full_width = 2 * kv_width
    page_rows = keys_values.reshape(PAGES, PAGE, full_width)
    ordered = jnp.zeros_like(page_rows).at[page_table].set(page_rows).reshape(TOKENS, full_width)
    padded = jnp.concatenate([ordered, jnp.zeros((KERNEL - STRIDE, full_width), jnp.bfloat16)], axis=0)
    padded = padded.astype(jnp.float32)
    depthwise = jnp.zeros((CROWS, full_width), jnp.float32)
    for offset in range(KERNEL):
        depthwise = depthwise + depth_kernel[offset][None, :] * padded[offset::STRIDE][:CROWS]
    depthwise = depthwise.astype(jnp.bfloat16)
    key_part = jnp.dot(depthwise[:, :kv_width], point_weight[0], preferred_element_type=jnp.float32)
    value_part = jnp.dot(depthwise[:, kv_width:], point_weight[1], preferred_element_type=jnp.float32)
    compressed = jnp.concatenate([key_part, value_part], axis=1).astype(jnp.bfloat16)
    kv_tier = compressed.reshape(PAGES, CR_PAGE, full_width)[page_table].reshape(CROWS, full_width)
    key_unit = unit_rows(compressed[:, :kv_width], KVH).astype(jnp.float32)
    value_rows = compressed[:, kv_width:].astype(jnp.float32).reshape(CROWS, KVH, HD)
    doc_ends = jnp.cumsum(doc_lengths)
    row_start = STRIDE * jnp.arange(CROWS, dtype=jnp.int32)

    def per_page(inputs):
        query_page, kv_page, logical = inputs
        position = logical * PAGE + jnp.arange(PAGE, dtype=jnp.int32)
        doc_start = lax.optimization_barrier(jnp.sum(jnp.where(doc_ends[None, :] <= position[:, None], doc_lengths[None, :], 0), axis=1))
        query_unit = unit_rows(query_page, QH).reshape(PAGE, KVH, GROUP, HD).astype(jnp.float32)
        own_unit = unit_rows(kv_page[:, :kv_width], KVH).astype(jnp.float32)
        own_value = kv_page[:, kv_width:].astype(jnp.float32).reshape(PAGE, KVH, HD)
        scores = jnp.einsum('tkgd,rkd->tkgr', query_unit, key_unit)
        visible = (row_start[None, :] >= doc_start[:, None]) & (row_start[None, :] + KERNEL - 1 < position[:, None])
        weights = jnp.where(visible[:, None, None, :], jnp.exp(SCORE_SCALE / HD * scores), 0.0)
        own_weight = jnp.exp(SCORE_SCALE / HD * jnp.einsum('tkgd,tkd->tkg', query_unit, own_unit))
        weight_sum = own_weight + lax.optimization_barrier(jnp.sum(weights, axis=3))
        weights_low = weights.astype(jnp.bfloat16).astype(jnp.float32)
        mixture = jnp.einsum('tkgr,rkd->tkgd', weights_low, value_rows, precision=lax.Precision.HIGHEST)
        mixture = mixture + own_weight[..., None] * own_value[:, :, None, :]
        return (mixture / weight_sum[..., None]).reshape(PAGE, QH * HD).astype(jnp.bfloat16)
    attended = lax.map(per_page, (queries.reshape(PAGES, PAGE, QH * HD), page_rows, page_table))
    return (attended.reshape(TOKENS, QH * HD), kv_tier)
```

```python
import functools
import math
import jax
import jax.numpy as jnp
from jax import lax
from jax.experimental import pallas as pl
from jax.experimental.pallas import tpu as pltpu
from jax.sharding import PartitionSpec as P

KVH = 8
HD = 128
QH = 32
GROUP = QH // KVH
KERNEL = 8
STRIDE = 4
PAGE = 64
SCORE_SCALE = 6.0
EXP2_SCALE = SCORE_SCALE / HD * math.log2(math.e)
KV = KVH * HD
CR = PAGE // STRIDE
SLOTS = 2
ROWS = SLOTS * CR
TOK = SLOTS * PAGE
CHUNK_BLOCKS = 8
MESH = pl.DeviceIdType.MESH


def unit(x):
    return x * lax.rsqrt(jnp.mean(x * x, axis=1, keepdims=True) + 1e-06)


class Spread:
    def __init__(self, buf, z_send, z_recv, y_send, y_recv, c_send, c_recv, steps):
        self.buf, self.steps = buf, steps
        self.sems = dict(z=(z_send, z_recv), y=(y_send, y_recv), c=(c_send, c_recv))
        me = lax.axis_index("ctx")
        self.c = lax.rem(me, 2)
        self.y = lax.rem(me // 2, 2)
        self.z = me // 4

    def index(self, z, y, c):
        return (z * 2 + y) * 2 + c

    def origin(self, k, y, c):
        return self.index(lax.rem(self.z + self.steps - k, self.steps), y, c)

    def copy(self, kind, i, origin, target):
        send, recv = self.sems[kind]
        return pltpu.make_async_remote_copy(
            src_ref=self.buf.at[origin], dst_ref=self.buf.at[origin], send_sem=send.at[i],
            recv_sem=recv.at[i], device_id={"ctx": target}, device_id_type=MESH)

    def z_target(self, k):
        return self.index(lax.rem(self.z + k, self.steps), self.y, self.c)

    def z_out(self, k):
        return self.copy("z", k, self.origin(0, self.y, self.c), self.z_target(k))

    def z_in(self, k):
        return self.copy("z", k, self.origin(k, self.y, self.c), self.z_target(k))

    def y_out(self, k):
        return self.copy("y", k, self.origin(k, self.y, self.c), self.index(self.z, 1 - self.y, self.c))

    def y_in(self, k):
        return self.copy("y", k, self.origin(k, 1 - self.y, self.c), self.index(self.z, 1 - self.y, self.c))

    def c_out(self, j):
        y = self.y if j < self.steps else 1 - self.y
        return self.copy("c", j, self.origin(j % self.steps, y, self.c), self.index(self.z, self.y, 1 - self.c))

    def c_in(self, j):
        y = self.y if j < self.steps else 1 - self.y
        return self.copy("c", j, self.origin(j % self.steps, y, 1 - self.c), self.index(self.z, self.y, 1 - self.c))

    def begin(self):
        self.y_out(0).start()
        for k in range(1, self.steps):
            self.z_out(k).start()
        self.c_out(0).start()

    def relay_z(self, k):
        self.z_in(k).wait_recv()
        self.y_out(k).start()
        self.c_out(k).start()

    def relay_y(self, k):
        self.y_in(k).wait_recv()
        self.c_out(self.steps + k).start()

    def wait_c(self, j):
        self.c_in(j).wait_recv()

    def finish(self):
        for k in range(1, self.steps):
            self.z_out(k).wait_send()
        for k in range(self.steps):
            self.y_out(k).wait_send()
        for j in range(2 * self.steps):
            self.c_out(j).wait_send()


def kernel(n, pages, q_hbm, kv_ref, dk_ref, w_hbm, pt_ref, dl_ref, att_ref, tier_ref,
           q_ref, w_ref, kvf, edges, blocks, own, qn, acc, den, tails, tails_comp, keys,
           load_sem, ez_s, ez_r, ey_s, ey_r, ec_s, ec_r, mz_s, mz_r, my_s, my_r, mc_s, mc_r):
    steps = n // 4
    me = lax.axis_index("ctx")
    load_w = pltpu.make_async_copy(w_hbm, w_ref, load_sem.at[0])
    load_q = pltpu.make_async_copy(q_hbm, q_ref, load_sem.at[1])
    load_w.start()
    load_q.start()
    edge = Spread(edges, ez_s, ez_r, ey_s, ey_r, ec_s, ec_r, steps)
    main = Spread(blocks, mz_s, mz_r, my_s, my_r, mc_s, mc_r, steps)

    barrier = pltpu.get_barrier_semaphore()
    for k in range(1, steps):
        pl.semaphore_signal(barrier, inc=1, device_id={"ctx": edge.z_target(k)}, device_id_type=MESH)
    pl.semaphore_signal(barrier, inc=1, device_id={"ctx": edge.index(edge.z, 1 - edge.y, edge.c)}, device_id_type=MESH)
    pl.semaphore_signal(barrier, inc=1, device_id={"ctx": edge.index(edge.z, edge.y, 1 - edge.c)}, device_id_type=MESH)

    firsts, seconds = [], []
    for t in range(2 * KVH):
        cols = slice(t * HD, (t + 1) * HD)
        kvf[t] = kv_ref[:, cols].astype(jnp.float32)
        first = jnp.zeros((ROWS, HD), jnp.float32)
        second = jnp.zeros((ROWS, HD), jnp.float32)
        for o in range(STRIDE):
            x = kvf[t, pl.ds(o, ROWS, stride=STRIDE), :]
            first = first + x * dk_ref[o:o + 1, cols]
            second = second + x * dk_ref[STRIDE + o:STRIDE + o + 1, cols]
        firsts.append(first)
        seconds.append(second)
    first = jnp.concatenate(firsts, axis=1)
    second = jnp.concatenate(seconds, axis=1)
    for s in range(SLOTS):
        last, head = s * CR + CR - 1, s * CR
        for half in range(2):
            cols = slice(half * KV, (half + 1) * KV)
            edges[me, 2 * s + half:2 * s + half + 1, :] = first[last:last + 1, cols]
            edges[me, 4 + 2 * s + half:5 + 2 * s + half, :] = second[head:head + 1, cols]
    pl.semaphore_wait(barrier, steps + 1)
    edge.begin()

    depthwise = (first + pltpu.roll(second, ROWS - 1, 0)).astype(jnp.bfloat16)
    load_w.wait()
    key_part = jnp.dot(depthwise[:, :KV], w_ref[0], preferred_element_type=jnp.float32).astype(jnp.bfloat16)
    value_part = jnp.dot(depthwise[:, KV:], w_ref[1], preferred_element_type=jnp.float32).astype(jnp.bfloat16)
    own[:, :KV] = key_part.astype(jnp.float32)
    own[:, KV:] = value_part.astype(jnp.float32)
    for g in range(KVH):
        blocks[me, :, g * HD:(g + 1) * HD] = unit(own[:, g * HD:(g + 1) * HD]).astype(jnp.bfloat16)
    blocks[me, :, KV:] = value_part
    main.begin()

    def queries_of(g):
        own_unit = unit(kvf[g]).astype(jnp.bfloat16).astype(jnp.float32)
        own_value = kvf[KVH + g]
        lane = lax.broadcasted_iota(jnp.int32, (TOK, HD), 1)
        for h in range(g * GROUP, (g + 1) * GROUP):
            rows = slice(h * TOK, (h + 1) * TOK)
            low = unit(q_ref[:, h * HD:(h + 1) * HD].astype(jnp.float32)).astype(jnp.bfloat16)
            qn[rows, :] = low
            score = jnp.sum(low.astype(jnp.float32) * own_unit, axis=1, keepdims=True)
            weight = jnp.exp2(EXP2_SCALE * score)
            acc[rows, :] = weight * own_value
            den[rows, :] = jnp.where(lane == 0, weight, 0.0)

    load_q.wait()
    for k in range(1, steps):
        edge.relay_z(k)
    queries_of(0)
    queries_of(1)
    for k in range(steps):
        edge.relay_y(k)
    queries_of(2)
    queries_of(3)
    for k in range(1, steps):
        main.relay_z(k)
        if k < 4:
            queries_of(3 + k)
    queries_of(7)
    for j in range(2 * steps):
        edge.wait_c(j)

    slot_col = lax.broadcasted_iota(jnp.int32, (pages, 4 * SLOTS * n), 0)
    line = lax.broadcasted_iota(jnp.int32, (pages, 4 * SLOTS * n), 1)
    kind = line % 8
    line_slot = (line // 8) * SLOTS + (kind // 2) % 2
    page_of_slot = jnp.zeros((pages, 4 * SLOTS * n), jnp.int32)
    page_of_line = jnp.zeros((pages, 4 * SLOTS * n), jnp.int32)
    for s in range(pages):
        page_of_slot = jnp.where(slot_col == s, pt_ref[s], page_of_slot)
        page_of_line = jnp.where(line_slot == s, pt_ref[s], page_of_line)
    take = ((kind < 4) & (slot_col == line_slot)) | ((kind >= 4) & (page_of_line == page_of_slot + 1))
    lines = edges[...].reshape(n * 8, KV)
    for half in range(2):
        pick = jnp.where(take & (kind % 2 == half), 1.0, 0.0)
        row = jnp.dot(pick, lines, preferred_element_type=jnp.float32, precision=lax.Precision.HIGHEST)
        part = jnp.dot(row.astype(jnp.bfloat16), w_ref[half], preferred_element_type=jnp.float32)
        part = part.astype(jnp.bfloat16).astype(jnp.float32)
        tails_comp[:, half * KV:(half + 1) * KV] = part
        if half == 0:
            for g in range(KVH):
                cols = slice(g * HD, (g + 1) * HD)
                tails[:, cols] = unit(part[:, cols]).astype(jnp.bfloat16).astype(jnp.float32)
        else:
            tails[:, KV:] = part

    row_id = lax.broadcasted_iota(jnp.int32, (ROWS, 2 * KV), 0)

    def with_tails(block, table, b):
        t0 = table[pl.ds(SLOTS * b, 1), :]
        t1 = table[pl.ds(SLOTS * b + 1, 1), :]
        return jnp.where(row_id == CR - 1, t0, jnp.where(row_id == 2 * CR - 1, t1, block)).astype(jnp.bfloat16)

    tier_ref[...] = with_tails(own[...], tails_comp, me)

    token = lax.broadcasted_iota(jnp.int32, (TOK, 1), 0)
    page_here = jnp.where(token < PAGE, pt_ref[SLOTS * me], pt_ref[SLOTS * me + 1])
    position = page_here * PAGE + token % PAGE
    doc_start = jnp.zeros((TOK, 1), jnp.int32)
    end = jnp.int32(0)
    for d in range(dl_ref.shape[0]):
        end = end + dl_ref[d]
        doc_start = doc_start + jnp.where(end <= position, dl_ref[d], 0)

    def attend(members):
        count = len(members) * ROWS
        lane = lax.broadcasted_iota(jnp.int32, (1, count), 1)
        page_of = jnp.zeros((1, count), jnp.int32)
        for i, b in enumerate(members):
            keys[i * ROWS:(i + 1) * ROWS, :] = with_tails(blocks[b].astype(jnp.float32), tails, b)
            for s in range(SLOTS):
                page_of = jnp.where(lane // CR == i * SLOTS + s, pt_ref[SLOTS * b + s], page_of)
        start = STRIDE * (page_of * CR + lane % CR)
        seen = jnp.where((start >= doc_start) & (start + KERNEL - 1 < position), 1.0, 0.0)
        for g in range(KVH):
            rows = slice(g * GROUP * TOK, (g + 1) * GROUP * TOK)
            key_block = keys[:count, g * HD:(g + 1) * HD]
            value_block = keys[:count, KV + g * HD:KV + (g + 1) * HD]
            score = lax.dot_general(qn[rows, :], key_block, (((1,), (1,)), ((), ())),
                                    preferred_element_type=jnp.float32)
            weight = jnp.exp2(EXP2_SCALE * score).reshape(GROUP, TOK, count) * seen[None]
            weight = weight.reshape(GROUP * TOK, count)
            acc[rows, :] += jnp.dot(weight.astype(jnp.bfloat16), value_block, preferred_element_type=jnp.float32)
            total = den[rows, :]
            for i in range(count // HD):
                total = total + weight[:, i * HD:(i + 1) * HD]
            den[rows, :] = total

    near = [main.origin(k, main.y, c) for k in range(steps) for c in (main.c, 1 - main.c)]
    far = [main.origin(k, 1 - main.y, c) for k in range(steps) for c in (main.c, 1 - main.c)]
    for j in range(steps):
        main.wait_c(j)
    for a in range(0, len(near), CHUNK_BLOCKS):
        attend(near[a:a + CHUNK_BLOCKS])
    for k in range(steps):
        main.relay_y(k)
    for k in range(steps):
        main.wait_c(steps + k)
    for a in range(0, len(far), CHUNK_BLOCKS):
        attend(far[a:a + CHUNK_BLOCKS])
    for h in range(QH):
        rows = slice(h * TOK, (h + 1) * TOK)
        total = jnp.sum(den[rows, :], axis=1, keepdims=True)
        att_ref[:, h * HD:(h + 1) * HD] = (acc[rows, :] * (1.0 / total)).astype(jnp.bfloat16)
    edge.finish()
    main.finish()


def shards(n, queries, keys_values, depth_kernel, point_weight, page_table, doc_lengths):
    pages = page_table.shape[0]
    steps = n // 4
    vmem = pl.BlockSpec(memory_space=pltpu.VMEM)
    hbm = pl.BlockSpec(memory_space=pl.ANY)
    smem = pl.BlockSpec(memory_space=pltpu.SMEM)
    dma = pltpu.SemaphoreType.DMA
    spread = [dma((steps,)), dma((steps,)), dma((steps,)), dma((steps,)), dma((2 * steps,)), dma((2 * steps,))]
    return pl.pallas_call(
        functools.partial(kernel, n, pages),
        out_shape=(jax.ShapeDtypeStruct((TOK, QH * HD), jnp.bfloat16),
                   jax.ShapeDtypeStruct((ROWS, 2 * KV), jnp.bfloat16)),
        in_specs=[hbm, vmem, vmem, hbm, smem, smem],
        out_specs=(vmem, vmem),
        scratch_shapes=[
            pltpu.VMEM((TOK, QH * HD), jnp.bfloat16),
            pltpu.VMEM((2, KV, KV), jnp.bfloat16),
            pltpu.VMEM((2 * KVH, TOK, HD), jnp.float32),
            pltpu.VMEM((n, 8, KV), jnp.float32),
            pltpu.VMEM((n, ROWS, 2 * KV), jnp.bfloat16),
            pltpu.VMEM((ROWS, 2 * KV), jnp.float32),
            pltpu.VMEM((QH * TOK, HD), jnp.bfloat16),
            pltpu.VMEM((QH * TOK, HD), jnp.float32),
            pltpu.VMEM((QH * TOK, HD), jnp.float32),
            pltpu.VMEM((pages, 2 * KV), jnp.float32),
            pltpu.VMEM((pages, 2 * KV), jnp.float32),
            pltpu.VMEM((CHUNK_BLOCKS * ROWS, 2 * KV), jnp.bfloat16),
            dma((2,)),
        ] + spread + spread,
        compiler_params=pltpu.CompilerParams(collective_id=0, has_side_effects=True),
    )(queries, keys_values, depth_kernel, point_weight, page_table, doc_lengths)


def solution(mesh):
    placed = (P(("grp", "ctx"), None), P(("grp", "ctx"), None), P(), P(), P("grp"), P("grp"))
    return jax.shard_map(
        functools.partial(shards, mesh.shape["ctx"]),
        mesh=mesh,
        in_specs=placed,
        out_specs=(P(("grp", "ctx"), None), P(("grp", "ctx"), None)),
        check_vma=False,
    )
```

```python
import functools
import math
import jax
import jax.numpy as jnp
from jax import lax
from jax.experimental import pallas as pl
from jax.experimental.pallas import tpu as pltpu
from jax.sharding import PartitionSpec as P

KVH = 8
HD = 128
QH = 32
GROUP = QH // KVH
KERNEL = 8
STRIDE = 4
PAGE = 64
SCORE_SCALE = 6.0
EXP2_SCALE = SCORE_SCALE / HD * math.log2(math.e)
KV = KVH * HD
CR = PAGE // STRIDE
SLOTS = 2
ROWS = SLOTS * CR
TOK = SLOTS * PAGE
CHUNK_BLOCKS = 8
PIECES = 4
PIECE = 2 * KV // PIECES
MESH = pl.DeviceIdType.MESH


def unit(x):
    return x * lax.rsqrt(jnp.mean(x * x, axis=1, keepdims=True) + 1e-06)


class Spread:
    def __init__(self, buf, z_send, z_recv, y_send, y_recv, c_send, c_recv, steps):
        self.buf, self.steps = buf, steps
        self.sems = dict(z=(z_send, z_recv), y=(y_send, y_recv), c=(c_send, c_recv))
        me = lax.axis_index("ctx")
        self.c = lax.rem(me, 2)
        self.y = lax.rem(me // 2, 2)
        self.z = me // 4

    def index(self, z, y, c):
        return (z * 2 + y) * 2 + c

    def origin(self, k, y, c):
        return self.index(lax.rem(self.z + self.steps - k, self.steps), y, c)

    def copy(self, kind, i, origin, target):
        send, recv = self.sems[kind]
        return pltpu.make_async_remote_copy(
            src_ref=self.buf.at[origin], dst_ref=self.buf.at[origin], send_sem=send.at[i],
            recv_sem=recv.at[i], device_id={"ctx": target}, device_id_type=MESH)

    def z_target(self, k):
        return self.index(lax.rem(self.z + k, self.steps), self.y, self.c)

    def z_out(self, k):
        return self.copy("z", k, self.origin(0, self.y, self.c), self.z_target(k))

    def z_in(self, k):
        return self.copy("z", k, self.origin(k, self.y, self.c), self.z_target(k))

    def y_out(self, k):
        return self.copy("y", k, self.origin(k, self.y, self.c), self.index(self.z, 1 - self.y, self.c))

    def y_in(self, k):
        return self.copy("y", k, self.origin(k, 1 - self.y, self.c), self.index(self.z, 1 - self.y, self.c))

    def c_out(self, j):
        y = self.y if j < self.steps else 1 - self.y
        return self.copy("c", j, self.origin(j % self.steps, y, self.c), self.index(self.z, self.y, 1 - self.c))

    def c_in(self, j):
        y = self.y if j < self.steps else 1 - self.y
        return self.copy("c", j, self.origin(j % self.steps, y, 1 - self.c), self.index(self.z, self.y, 1 - self.c))

    def begin(self):
        self.y_out(0).start()
        for k in range(1, self.steps):
            self.z_out(k).start()
        self.c_out(0).start()

    def relay_z(self, k):
        self.z_in(k).wait_recv()
        self.y_out(k).start()
        self.c_out(k).start()

    def relay_y(self, k):
        self.y_in(k).wait_recv()
        self.c_out(self.steps + k).start()

    def wait_c(self, j):
        self.c_in(j).wait_recv()

    def finish(self):
        for k in range(1, self.steps):
            self.z_out(k).wait_send()
        for k in range(self.steps):
            self.y_out(k).wait_send()
        for j in range(2 * self.steps):
            self.c_out(j).wait_send()


class Ring:
    def __init__(self, buf, chips, r_send, r_recv, l_send, l_recv, c_send, c_recv):
        self.buf, self.chips, self.half = buf, chips, chips // 2
        self.sems = dict(r=(r_send, r_recv), l=(l_send, l_recv), c=(c_send, c_recv))
        me = lax.axis_index("ctx")
        self.me, self.c = me, lax.rem(me, 2)
        self.snake = chips <= 8
        chip = me // 2
        if self.snake:
            z, y = chip // 2, lax.rem(chip, 2)
            chip = z + y * (chips - 1 - 2 * z)
        self.r = chip

    def at(self, d, other=False):
        r = lax.rem(self.r + d + self.chips, self.chips)
        if self.snake:
            high = r // self.half
            r = 2 * (r + high * (self.chips - 1 - 2 * r)) + high
        return r * 2 + (1 - self.c if other else self.c)

    def copy(self, kind, i, origin, p, target):
        send, recv = self.sems[kind]
        piece = self.buf.at[origin, p]
        return pltpu.make_async_remote_copy(
            src_ref=piece, dst_ref=piece, send_sem=send.at[i], recv_sem=recv.at[i],
            device_id={"ctx": target}, device_id_type=MESH)

    def right(self, d, p, arriving=False):
        return self.copy("r", (d - arriving) * PIECES + p, self.at(-d), p, self.at(1))

    def left(self, d, p, arriving=False):
        return self.copy("l", (d - arriving) * PIECES + p, self.at(d), p, self.at(-1))

    def core(self, d, p, arriving=False):
        return self.copy("c", (d % self.chips) * PIECES + p, self.at(d, arriving), p, self.at(0, True))

    def goes_right(self, d, p):
        return d < self.half - 1 or (d == self.half - 1 and p % 2 == 0)

    def goes_left(self, d, p):
        return d < self.half - 1 or (d == self.half - 1 and p % 2 == 1)

    def begin(self, p):
        if self.goes_right(0, p):
            self.right(0, p).start()
        if self.goes_left(0, p):
            self.left(0, p).start()
        self.core(0, p).start()

    def relay(self, d, p):
        if self.goes_right(d - 1, p):
            self.right(d, p, True).wait_recv()
            if self.goes_right(d, p):
                self.right(d, p).start()
            self.core(-d, p).start()
        if self.goes_left(d - 1, p):
            self.left(d, p, True).wait_recv()
            if self.goes_left(d, p):
                self.left(d, p).start()
            self.core(d, p).start()

    def wait_core(self, d):
        for p in range(PIECES):
            self.core(d, p, True).wait_recv()

    def finish(self):
        for d in range(self.half):
            for p in range(PIECES):
                if self.goes_right(d, p):
                    self.right(d, p).wait_send()
                if self.goes_left(d, p):
                    self.left(d, p).wait_send()
        for d in range(self.chips):
            for p in range(PIECES):
                self.core(d, p).wait_send()


def kernel(n, pages, q_hbm, kv_ref, dk_ref, w_hbm, pt_ref, dl_ref, att_ref, tier_ref,
           q_ref, w_ref, kvf, edges, blocks, own, qn, acc, den, tails, tails_comp, keys,
           load_sem, ez_s, ez_r, ey_s, ey_r, ec_s, ec_r, *ring_sems):
    steps = n // 4
    me = lax.axis_index("ctx")
    halves = [1 - p // 2 for p in range(PIECES)]
    inside = [slice(p % 2 * PIECE, (p % 2 + 1) * PIECE) for p in range(PIECES)]
    across = [slice(half * KV + p % 2 * PIECE, half * KV + (p % 2 + 1) * PIECE) for p, half in enumerate(halves)]
    load_w = [pltpu.make_async_copy(w_hbm.at[halves[p], :, inside[p]], w_ref.at[p], load_sem.at[p]) for p in range(PIECES)]
    load_q = pltpu.make_async_copy(q_hbm, q_ref, load_sem.at[PIECES])
    for load in load_w:
        load.start()
    load_q.start()
    edge = Spread(edges, ez_s, ez_r, ey_s, ey_r, ec_s, ec_r, steps)
    main = Ring(blocks, n // 2, *ring_sems)

    barrier = pltpu.get_barrier_semaphore()
    for k in range(1, steps):
        pl.semaphore_signal(barrier, inc=1, device_id={"ctx": edge.z_target(k)}, device_id_type=MESH)
    pl.semaphore_signal(barrier, inc=1, device_id={"ctx": edge.index(edge.z, 1 - edge.y, edge.c)}, device_id_type=MESH)
    pl.semaphore_signal(barrier, inc=1, device_id={"ctx": edge.index(edge.z, edge.y, 1 - edge.c)}, device_id_type=MESH)
    for side in (-1, 1):
        pl.semaphore_signal(barrier, inc=1, device_id={"ctx": main.at(side)}, device_id_type=MESH)

    firsts, seconds = [], []
    for t in range(2 * KVH):
        cols = slice(t * HD, (t + 1) * HD)
        kvf[t] = kv_ref[:, cols].astype(jnp.float32)
        first = jnp.zeros((ROWS, HD), jnp.float32)
        second = jnp.zeros((ROWS, HD), jnp.float32)
        for o in range(STRIDE):
            x = kvf[t, pl.ds(o, ROWS, stride=STRIDE), :]
            first = first + x * dk_ref[o:o + 1, cols]
            second = second + x * dk_ref[STRIDE + o:STRIDE + o + 1, cols]
        firsts.append(first)
        seconds.append(second)
    first = jnp.concatenate(firsts, axis=1)
    second = jnp.concatenate(seconds, axis=1)
    for s in range(SLOTS):
        last, head = s * CR + CR - 1, s * CR
        for half in range(2):
            cols = slice(half * KV, (half + 1) * KV)
            edges[me, 2 * s + half:2 * s + half + 1, :] = first[last:last + 1, cols]
            edges[me, 4 + 2 * s + half:5 + 2 * s + half, :] = second[head:head + 1, cols]
    pl.semaphore_wait(barrier, steps + 3)
    edge.begin()

    depthwise = (first + pltpu.roll(second, ROWS - 1, 0)).astype(jnp.bfloat16)
    for p in range(PIECES):
        load_w[p].wait()
        taken = depthwise[:, halves[p] * KV:(halves[p] + 1) * KV]
        part = jnp.dot(taken, w_ref[p], preferred_element_type=jnp.float32).astype(jnp.bfloat16)
        wide = part.astype(jnp.float32)
        own[:, across[p]] = wide
        if halves[p]:
            blocks[me, p] = part
        else:
            for g in range(PIECE // HD):
                cols = slice(g * HD, (g + 1) * HD)
                blocks[me, p, :, cols] = unit(wide[:, cols]).astype(jnp.bfloat16)
        main.begin(p)

    def queries_of(g):
        own_unit = unit(kvf[g]).astype(jnp.bfloat16).astype(jnp.float32)
        own_value = kvf[KVH + g]
        lane = lax.broadcasted_iota(jnp.int32, (TOK, HD), 1)
        for h in range(g * GROUP, (g + 1) * GROUP):
            rows = slice(h * TOK, (h + 1) * TOK)
            low = unit(q_ref[:, h * HD:(h + 1) * HD].astype(jnp.float32)).astype(jnp.bfloat16)
            qn[rows, :] = low
            score = jnp.sum(low.astype(jnp.float32) * own_unit, axis=1, keepdims=True)
            weight = jnp.exp2(EXP2_SCALE * score)
            acc[rows, :] = weight * own_value
            den[rows, :] = jnp.where(lane == 0, weight, 0.0)

    load_q.wait()
    for k in range(1, steps):
        edge.relay_z(k)
    for g in range(3):
        queries_of(g)
    for k in range(steps):
        edge.relay_y(k)
    for p in range(PIECES):
        main.relay(1, p)
        queries_of(3 + p)
    queries_of(7)
    for p in range(PIECES):
        main.relay(2, p)
    for j in range(2 * steps):
        edge.wait_c(j)

    slot_col = lax.broadcasted_iota(jnp.int32, (pages, 4 * SLOTS * n), 0)
    line = lax.broadcasted_iota(jnp.int32, (pages, 4 * SLOTS * n), 1)
    kind = line % 8
    line_slot = (line // 8) * SLOTS + (kind // 2) % 2
    page_of_slot = jnp.zeros((pages, 4 * SLOTS * n), jnp.int32)
    page_of_line = jnp.zeros((pages, 4 * SLOTS * n), jnp.int32)
    for s in range(pages):
        page_of_slot = jnp.where(slot_col == s, pt_ref[s], page_of_slot)
        page_of_line = jnp.where(line_slot == s, pt_ref[s], page_of_line)
    take = ((kind < 4) & (slot_col == line_slot)) | ((kind >= 4) & (page_of_line == page_of_slot + 1))
    lines = edges[...].reshape(n * 8, KV)
    rows_last = []
    for half in range(2):
        pick = jnp.where(take & (kind % 2 == half), 1.0, 0.0)
        row = jnp.dot(pick, lines, preferred_element_type=jnp.float32, precision=lax.Precision.HIGHEST)
        rows_last.append(row.astype(jnp.bfloat16))
    for p in range(PIECES):
        part = jnp.dot(rows_last[halves[p]], w_ref[p], preferred_element_type=jnp.float32)
        part = part.astype(jnp.bfloat16).astype(jnp.float32)
        tails_comp[:, across[p]] = part
        if halves[p]:
            tails[:, across[p]] = part
        else:
            for g in range(PIECE // HD):
                cols = slice(g * HD, (g + 1) * HD)
                tails[:, p % 2 * PIECE + g * HD:p % 2 * PIECE + (g + 1) * HD] = (
                    unit(part[:, cols]).astype(jnp.bfloat16).astype(jnp.float32))

    row_id = lax.broadcasted_iota(jnp.int32, (ROWS, PIECE), 0)

    def with_tails(block, table, b, cols):
        t0 = table[pl.ds(SLOTS * b, 1), cols]
        t1 = table[pl.ds(SLOTS * b + 1, 1), cols]
        return jnp.where(row_id == CR - 1, t0, jnp.where(row_id == 2 * CR - 1, t1, block)).astype(jnp.bfloat16)

    for p in range(PIECES):
        tier_ref[:, across[p]] = with_tails(own[:, across[p]], tails_comp, me, across[p])

    token = lax.broadcasted_iota(jnp.int32, (TOK, 1), 0)
    page_here = jnp.where(token < PAGE, pt_ref[SLOTS * me], pt_ref[SLOTS * me + 1])
    position = page_here * PAGE + token % PAGE
    doc_start = jnp.zeros((TOK, 1), jnp.int32)
    end = jnp.int32(0)
    for d in range(dl_ref.shape[0]):
        end = end + dl_ref[d]
        doc_start = doc_start + jnp.where(end <= position, dl_ref[d], 0)

    def attend(members):
        count = len(members) * ROWS
        lane = lax.broadcasted_iota(jnp.int32, (1, count), 1)
        page_of = jnp.zeros((1, count), jnp.int32)
        for i, b in enumerate(members):
            for p in range(PIECES):
                keys[i * ROWS:(i + 1) * ROWS, across[p]] = with_tails(blocks[b, p].astype(jnp.float32), tails, b, across[p])
            for s in range(SLOTS):
                page_of = jnp.where(lane // CR == i * SLOTS + s, pt_ref[SLOTS * b + s], page_of)
        start = STRIDE * (page_of * CR + lane % CR)
        seen = jnp.where((start >= doc_start) & (start + KERNEL - 1 < position), 1.0, 0.0)
        for g in range(KVH):
            rows = slice(g * GROUP * TOK, (g + 1) * GROUP * TOK)
            key_block = keys[:count, g * HD:(g + 1) * HD]
            value_block = keys[:count, KV + g * HD:KV + (g + 1) * HD]
            score = lax.dot_general(qn[rows, :], key_block, (((1,), (1,)), ((), ())),
                                    preferred_element_type=jnp.float32)
            weight = jnp.exp2(EXP2_SCALE * score).reshape(GROUP, TOK, count) * seen[None]
            weight = weight.reshape(GROUP * TOK, count)
            acc[rows, :] += jnp.dot(weight.astype(jnp.bfloat16), value_block, preferred_element_type=jnp.float32)
            total = den[rows, :]
            for i in range(count // HD):
                total = total + weight[:, i * HD:(i + 1) * HD]
            den[rows, :] = total

    half = n // 4
    ds = [0]
    for d in range(1, half):
        ds += [-d, d]
    ds.append(half)
    relayed, chips_of_chunk = 2, CHUNK_BLOCKS // 2
    for a in range(0, len(ds), chips_of_chunk):
        part = ds[a:a + chips_of_chunk]
        while relayed < max(abs(d) for d in part):
            relayed += 1
            for p in range(PIECES):
                main.relay(relayed, p)
        for d in part:
            main.wait_core(d)
        attend([main.at(d, other) for d in part for other in (False, True)])
    for h in range(QH):
        rows = slice(h * TOK, (h + 1) * TOK)
        total = jnp.sum(den[rows, :], axis=1, keepdims=True)
        att_ref[:, h * HD:(h + 1) * HD] = (acc[rows, :] * (1.0 / total)).astype(jnp.bfloat16)
    edge.finish()
    main.finish()


def shards(n, queries, keys_values, depth_kernel, point_weight, page_table, doc_lengths):
    pages = page_table.shape[0]
    steps = n // 4
    vmem = pl.BlockSpec(memory_space=pltpu.VMEM)
    hbm = pl.BlockSpec(memory_space=pl.ANY)
    smem = pl.BlockSpec(memory_space=pltpu.SMEM)
    dma = pltpu.SemaphoreType.DMA
    spread = [dma((steps,)), dma((steps,)), dma((steps,)), dma((steps,)), dma((2 * steps,)), dma((2 * steps,))]
    ring = [dma((steps * PIECES,))] * 4 + [dma((n // 2 * PIECES,))] * 2
    return pl.pallas_call(
        functools.partial(kernel, n, pages),
        out_shape=(jax.ShapeDtypeStruct((TOK, QH * HD), jnp.bfloat16),
                   jax.ShapeDtypeStruct((ROWS, 2 * KV), jnp.bfloat16)),
        in_specs=[hbm, vmem, vmem, hbm, smem, smem],
        out_specs=(vmem, vmem),
        scratch_shapes=[
            pltpu.VMEM((TOK, QH * HD), jnp.bfloat16),
            pltpu.VMEM((PIECES, KV, PIECE), jnp.bfloat16),
            pltpu.VMEM((2 * KVH, TOK, HD), jnp.float32),
            pltpu.VMEM((n, 8, KV), jnp.float32),
            pltpu.VMEM((n, PIECES, ROWS, PIECE), jnp.bfloat16),
            pltpu.VMEM((ROWS, 2 * KV), jnp.float32),
            pltpu.VMEM((QH * TOK, HD), jnp.bfloat16),
            pltpu.VMEM((QH * TOK, HD), jnp.float32),
            pltpu.VMEM((QH * TOK, HD), jnp.float32),
            pltpu.VMEM((pages, 2 * KV), jnp.float32),
            pltpu.VMEM((pages, 2 * KV), jnp.float32),
            pltpu.VMEM((CHUNK_BLOCKS * ROWS, 2 * KV), jnp.bfloat16),
            dma((PIECES + 1,)),
        ] + spread + ring,
        compiler_params=pltpu.CompilerParams(collective_id=0, has_side_effects=True),
    )(queries, keys_values, depth_kernel, point_weight, page_table, doc_lengths)


def solution(mesh):
    placed = (P(("grp", "ctx"), None), P(("grp", "ctx"), None), P(), P(), P("grp"), P("grp"))
    return jax.shard_map(
        functools.partial(shards, mesh.shape["ctx"]),
        mesh=mesh,
        in_specs=placed,
        out_specs=(P(("grp", "ctx"), None), P(("grp", "ctx"), None)),
        check_vma=False,
    )
```

```python
import functools
import math
import jax
import jax.numpy as jnp
from jax import lax
from jax.experimental import pallas as pl
from jax.experimental.pallas import tpu as pltpu
from jax.sharding import PartitionSpec as P

KVH = 8
HD = 128
QH = 32
GROUP = QH // KVH
KERNEL = 8
STRIDE = 4
PAGE = 64
SCORE_SCALE = 6.0
EXP2_SCALE = SCORE_SCALE / HD * math.log2(math.e)
KV = KVH * HD
CR = PAGE // STRIDE
SLOTS = 2
ROWS = SLOTS * CR
TOK = SLOTS * PAGE
CHUNK_BLOCKS = 8
PIECES = 4
PIECE = 2 * KV // PIECES
MESH = pl.DeviceIdType.MESH


def unit(x):
    return x * lax.rsqrt(jnp.mean(x * x, axis=1, keepdims=True) + 1e-06)


class Spread:
    def __init__(self, buf, z_send, z_recv, y_send, y_recv, c_send, c_recv, steps):
        self.buf, self.steps = buf, steps
        self.sems = dict(z=(z_send, z_recv), y=(y_send, y_recv), c=(c_send, c_recv))
        me = lax.axis_index("ctx")
        self.c = lax.rem(me, 2)
        self.y = lax.rem(me // 2, 2)
        self.z = me // 4

    def index(self, z, y, c):
        return (z * 2 + y) * 2 + c

    def origin(self, k, y, c):
        return self.index(lax.rem(self.z + self.steps - k, self.steps), y, c)

    def copy(self, kind, i, origin, target):
        send, recv = self.sems[kind]
        return pltpu.make_async_remote_copy(
            src_ref=self.buf.at[origin], dst_ref=self.buf.at[origin], send_sem=send.at[i],
            recv_sem=recv.at[i], device_id={"ctx": target}, device_id_type=MESH)

    def z_target(self, k):
        return self.index(lax.rem(self.z + k, self.steps), self.y, self.c)

    def z_out(self, k):
        return self.copy("z", k, self.origin(0, self.y, self.c), self.z_target(k))

    def z_in(self, k):
        return self.copy("z", k, self.origin(k, self.y, self.c), self.z_target(k))

    def y_out(self, k):
        return self.copy("y", k, self.origin(k, self.y, self.c), self.index(self.z, 1 - self.y, self.c))

    def y_in(self, k):
        return self.copy("y", k, self.origin(k, 1 - self.y, self.c), self.index(self.z, 1 - self.y, self.c))

    def c_out(self, j):
        y = self.y if j < self.steps else 1 - self.y
        return self.copy("c", j, self.origin(j % self.steps, y, self.c), self.index(self.z, self.y, 1 - self.c))

    def c_in(self, j):
        y = self.y if j < self.steps else 1 - self.y
        return self.copy("c", j, self.origin(j % self.steps, y, 1 - self.c), self.index(self.z, self.y, 1 - self.c))

    def begin(self):
        self.y_out(0).start()
        for k in range(1, self.steps):
            self.z_out(k).start()
        self.c_out(0).start()

    def relay_z(self, k):
        self.z_in(k).wait_recv()
        self.y_out(k).start()
        self.c_out(k).start()

    def relay_y(self, k):
        self.y_in(k).wait_recv()
        self.c_out(self.steps + k).start()

    def wait_c(self, j):
        self.c_in(j).wait_recv()

    def finish(self):
        for k in range(1, self.steps):
            self.z_out(k).wait_send()
        for k in range(self.steps):
            self.y_out(k).wait_send()
        for j in range(2 * self.steps):
            self.c_out(j).wait_send()


class Ring:
    def __init__(self, buf, chips, r_send, r_recv, l_send, l_recv, c_send, c_recv):
        self.buf, self.chips, self.half = buf, chips, chips // 2
        self.sems = dict(r=(r_send, r_recv), l=(l_send, l_recv), c=(c_send, c_recv))
        me = lax.axis_index("ctx")
        self.me, self.c = me, lax.rem(me, 2)
        self.snake = chips <= 8
        chip = me // 2
        if self.snake:
            z, y = chip // 2, lax.rem(chip, 2)
            chip = z + y * (chips - 1 - 2 * z)
        self.r = chip

    def at(self, d, other=False):
        r = lax.rem(self.r + d + self.chips, self.chips)
        if self.snake:
            high = r // self.half
            r = 2 * (r + high * (self.chips - 1 - 2 * r)) + high
        return r * 2 + (1 - self.c if other else self.c)

    def copy(self, kind, i, origin, p, target):
        send, recv = self.sems[kind]
        piece = self.buf.at[origin, p]
        return pltpu.make_async_remote_copy(
            src_ref=piece, dst_ref=piece, send_sem=send.at[i], recv_sem=recv.at[i],
            device_id={"ctx": target}, device_id_type=MESH)

    def right(self, d, p, arriving=False):
        return self.copy("r", (d - arriving) * PIECES + p, self.at(-d), p, self.at(1))

    def left(self, d, p, arriving=False):
        return self.copy("l", (d - arriving) * PIECES + p, self.at(d), p, self.at(-1))

    def core(self, d, p, arriving=False):
        return self.copy("c", (d % self.chips) * PIECES + p, self.at(d, arriving), p, self.at(0, True))

    def goes_right(self, d, p):
        return d < self.half - 1 or (d == self.half - 1 and p % 2 == 0)

    def goes_left(self, d, p):
        return d < self.half - 1 or (d == self.half - 1 and p % 2 == 1)

    def begin(self, p):
        if self.goes_right(0, p):
            self.right(0, p).start()
        if self.goes_left(0, p):
            self.left(0, p).start()
        self.core(0, p).start()

    def relay(self, d, p):
        if self.goes_right(d - 1, p):
            self.right(d, p, True).wait_recv()
            if self.goes_right(d, p):
                self.right(d, p).start()
            self.core(-d, p).start()
        if self.goes_left(d - 1, p):
            self.left(d, p, True).wait_recv()
            if self.goes_left(d, p):
                self.left(d, p).start()
            self.core(d, p).start()

    def wait_core(self, d):
        for p in range(PIECES):
            self.core(d, p, True).wait_recv()

    def finish(self):
        for d in range(self.half):
            for p in range(PIECES):
                if self.goes_right(d, p):
                    self.right(d, p).wait_send()
                if self.goes_left(d, p):
                    self.left(d, p).wait_send()
        for d in range(self.chips):
            for p in range(PIECES):
                self.core(d, p).wait_send()


def kernel(n, pages, q_hbm, kv_hbm, dk_hbm, w_hbm, pt_ref, dl_ref, att_ref, tier_ref,
           q_ref, kv_ref, dk_ref, w_ref, kvf, edges, blocks, own, qn, acc, den, tails, tails_comp, keys,
           load_sem, ez_s, ez_r, ey_s, ey_r, ec_s, ec_r, *ring_sems):
    steps = n // 4
    me = lax.axis_index("ctx")
    halves = [1 - p // 2 for p in range(PIECES)]
    inside = [slice(p % 2 * PIECE, (p % 2 + 1) * PIECE) for p in range(PIECES)]
    across = [slice(half * KV + p % 2 * PIECE, half * KV + (p % 2 + 1) * PIECE) for p, half in enumerate(halves)]
    load_w = [pltpu.make_async_copy(w_hbm.at[halves[p], :, inside[p]], w_ref.at[p], load_sem.at[p]) for p in range(PIECES)]
    load_q = pltpu.make_async_copy(q_hbm, q_ref, load_sem.at[PIECES])
    load_kv = pltpu.make_async_copy(kv_hbm, kv_ref, load_sem.at[PIECES + 1])
    load_dk = pltpu.make_async_copy(dk_hbm, dk_ref, load_sem.at[PIECES + 2])
    for load in [load_kv, load_dk] + load_w:
        load.start()
    load_q.start()
    edge = Spread(edges, ez_s, ez_r, ey_s, ey_r, ec_s, ec_r, steps)
    main = Ring(blocks, n // 2, *ring_sems)

    barrier = pltpu.get_barrier_semaphore()
    for k in range(1, steps):
        pl.semaphore_signal(barrier, inc=1, device_id={"ctx": edge.z_target(k)}, device_id_type=MESH)
    pl.semaphore_signal(barrier, inc=1, device_id={"ctx": edge.index(edge.z, 1 - edge.y, edge.c)}, device_id_type=MESH)
    pl.semaphore_signal(barrier, inc=1, device_id={"ctx": edge.index(edge.z, edge.y, 1 - edge.c)}, device_id_type=MESH)
    for side in (-1, 1):
        pl.semaphore_signal(barrier, inc=1, device_id={"ctx": main.at(side)}, device_id_type=MESH)

    load_kv.wait()
    load_dk.wait()
    firsts, seconds = [], []
    for t in range(2 * KVH):
        cols = slice(t * HD, (t + 1) * HD)
        kvf[t] = kv_ref[:, cols].astype(jnp.float32)
        first = jnp.zeros((ROWS, HD), jnp.float32)
        second = jnp.zeros((ROWS, HD), jnp.float32)
        for o in range(STRIDE):
            x = kvf[t, pl.ds(o, ROWS, stride=STRIDE), :]
            first = first + x * dk_ref[o:o + 1, cols]
            second = second + x * dk_ref[STRIDE + o:STRIDE + o + 1, cols]
        firsts.append(first)
        seconds.append(second)
    first = jnp.concatenate(firsts, axis=1)
    second = jnp.concatenate(seconds, axis=1)
    for s in range(SLOTS):
        last, head = s * CR + CR - 1, s * CR
        for half in range(2):
            cols = slice(half * KV, (half + 1) * KV)
            edges[me, 2 * s + half:2 * s + half + 1, :] = first[last:last + 1, cols]
            edges[me, 4 + 2 * s + half:5 + 2 * s + half, :] = second[head:head + 1, cols]
    pl.semaphore_wait(barrier, steps + 3)
    edge.begin()

    depthwise = (first + pltpu.roll(second, ROWS - 1, 0)).astype(jnp.bfloat16)
    for p in range(PIECES):
        load_w[p].wait()
        taken = depthwise[:, halves[p] * KV:(halves[p] + 1) * KV]
        part = jnp.dot(taken, w_ref[p], preferred_element_type=jnp.float32).astype(jnp.bfloat16)
        wide = part.astype(jnp.float32)
        own[:, across[p]] = wide
        if halves[p]:
            blocks[me, p] = part
        else:
            for g in range(PIECE // HD):
                cols = slice(g * HD, (g + 1) * HD)
                blocks[me, p, :, cols] = unit(wide[:, cols]).astype(jnp.bfloat16)
        main.begin(p)

    def queries_of(g):
        own_unit = unit(kvf[g]).astype(jnp.bfloat16).astype(jnp.float32)
        own_value = kvf[KVH + g]
        lane = lax.broadcasted_iota(jnp.int32, (TOK, HD), 1)
        for h in range(g * GROUP, (g + 1) * GROUP):
            rows = slice(h * TOK, (h + 1) * TOK)
            low = unit(q_ref[:, h * HD:(h + 1) * HD].astype(jnp.float32)).astype(jnp.bfloat16)
            qn[rows, :] = low
            score = jnp.sum(low.astype(jnp.float32) * own_unit, axis=1, keepdims=True)
            weight = jnp.exp2(EXP2_SCALE * score)
            acc[rows, :] = weight * own_value
            den[rows, :] = jnp.where(lane == 0, weight, 0.0)

    load_q.wait()
    queries_of(0)
    queries_of(1)
    for k in range(1, steps):
        edge.relay_z(k)
    for p in range(PIECES):
        main.relay(1, p)
        queries_of(2 + p)
    for k in range(steps):
        edge.relay_y(k)
    for p in range(PIECES):
        main.relay(2, p)
    queries_of(6)
    queries_of(7)
    for p in range(PIECES):
        main.relay(3, p)
    for j in range(2 * steps):
        edge.wait_c(j)

    slot_col = lax.broadcasted_iota(jnp.int32, (pages, 4 * SLOTS * n), 0)
    line = lax.broadcasted_iota(jnp.int32, (pages, 4 * SLOTS * n), 1)
    kind = line % 8
    line_slot = (line // 8) * SLOTS + (kind // 2) % 2
    page_of_slot = jnp.zeros((pages, 4 * SLOTS * n), jnp.int32)
    page_of_line = jnp.zeros((pages, 4 * SLOTS * n), jnp.int32)
    for s in range(pages):
        page_of_slot = jnp.where(slot_col == s, pt_ref[s], page_of_slot)
        page_of_line = jnp.where(line_slot == s, pt_ref[s], page_of_line)
    take = ((kind < 4) & (slot_col == line_slot)) | ((kind >= 4) & (page_of_line == page_of_slot + 1))
    lines = edges[...].reshape(n * 8, KV)
    rows_last = []
    for half in range(2):
        pick = jnp.where(take & (kind % 2 == half), 1.0, 0.0)
        row = jnp.dot(pick, lines, preferred_element_type=jnp.float32, precision=lax.Precision.HIGHEST)
        rows_last.append(row.astype(jnp.bfloat16))
    for p in range(PIECES):
        part = jnp.dot(rows_last[halves[p]], w_ref[p], preferred_element_type=jnp.float32)
        part = part.astype(jnp.bfloat16).astype(jnp.float32)
        tails_comp[:, across[p]] = part
        if halves[p]:
            tails[:, across[p]] = part
        else:
            for g in range(PIECE // HD):
                cols = slice(g * HD, (g + 1) * HD)
                tails[:, p % 2 * PIECE + g * HD:p % 2 * PIECE + (g + 1) * HD] = (
                    unit(part[:, cols]).astype(jnp.bfloat16).astype(jnp.float32))

    row_id = lax.broadcasted_iota(jnp.int32, (ROWS, PIECE), 0)

    def with_tails(block, table, b, cols):
        t0 = table[pl.ds(SLOTS * b, 1), cols]
        t1 = table[pl.ds(SLOTS * b + 1, 1), cols]
        return jnp.where(row_id == CR - 1, t0, jnp.where(row_id == 2 * CR - 1, t1, block)).astype(jnp.bfloat16)

    for p in range(PIECES):
        tier_ref[:, across[p]] = with_tails(own[:, across[p]], tails_comp, me, across[p])

    token = lax.broadcasted_iota(jnp.int32, (TOK, 1), 0)
    page_here = jnp.where(token < PAGE, pt_ref[SLOTS * me], pt_ref[SLOTS * me + 1])
    position = page_here * PAGE + token % PAGE
    doc_start = jnp.zeros((TOK, 1), jnp.int32)
    end = jnp.int32(0)
    for d in range(dl_ref.shape[0]):
        end = end + dl_ref[d]
        doc_start = doc_start + jnp.where(end <= position, dl_ref[d], 0)

    def attend(members):
        count = len(members) * ROWS
        lane = lax.broadcasted_iota(jnp.int32, (1, count), 1)
        page_of = jnp.zeros((1, count), jnp.int32)
        for i, b in enumerate(members):
            for p in range(PIECES):
                keys[i * ROWS:(i + 1) * ROWS, across[p]] = with_tails(blocks[b, p].astype(jnp.float32), tails, b, across[p])
            for s in range(SLOTS):
                page_of = jnp.where(lane // CR == i * SLOTS + s, pt_ref[SLOTS * b + s], page_of)
        start = STRIDE * (page_of * CR + lane % CR)
        seen = jnp.where((start >= doc_start) & (start + KERNEL - 1 < position), 1.0, 0.0)
        for g in range(KVH):
            rows = slice(g * GROUP * TOK, (g + 1) * GROUP * TOK)
            key_block = keys[:count, g * HD:(g + 1) * HD]
            value_block = keys[:count, KV + g * HD:KV + (g + 1) * HD]
            score = lax.dot_general(qn[rows, :], key_block, (((1,), (1,)), ((), ())),
                                    preferred_element_type=jnp.float32)
            weight = jnp.exp2(EXP2_SCALE * score).reshape(GROUP, TOK, count) * seen[None]
            weight = weight.reshape(GROUP * TOK, count)
            acc[rows, :] += jnp.dot(weight.astype(jnp.bfloat16), value_block, preferred_element_type=jnp.float32)
            total = den[rows, :]
            for i in range(count // HD):
                total = total + weight[:, i * HD:(i + 1) * HD]
            den[rows, :] = total

    half = n // 4
    ds = [0]
    for d in range(1, half):
        ds += [-d, d]
    ds.append(half)
    relayed, chips_of_chunk = 3, CHUNK_BLOCKS // 2
    for a in range(0, len(ds), chips_of_chunk):
        part = ds[a:a + chips_of_chunk]
        while relayed < max(abs(d) for d in part):
            relayed += 1
            for p in range(PIECES):
                main.relay(relayed, p)
        for d in part:
            main.wait_core(d)
        attend([main.at(d, other) for d in part for other in (False, True)])
    for h in range(QH):
        rows = slice(h * TOK, (h + 1) * TOK)
        total = jnp.sum(den[rows, :], axis=1, keepdims=True)
        att_ref[:, h * HD:(h + 1) * HD] = (acc[rows, :] * (1.0 / total)).astype(jnp.bfloat16)
    edge.finish()
    main.finish()


def place(att_in, tier_in, att_out, tier_out, sems):
    first = pltpu.make_async_copy(att_in, att_out, sems.at[0])
    second = pltpu.make_async_copy(tier_in, tier_out, sems.at[1])
    first.start()
    second.start()
    first.wait()
    second.wait()


def shards(n, queries, keys_values, depth_kernel, point_weight, page_table, doc_lengths):
    pages = page_table.shape[0]
    steps = n // 4
    held = pl.BlockSpec(memory_space=pltpu.HBM)
    vmem = pl.BlockSpec(memory_space=pltpu.VMEM)
    hbm = pl.BlockSpec(memory_space=pl.ANY)
    smem = pl.BlockSpec(memory_space=pltpu.SMEM)
    dma = pltpu.SemaphoreType.DMA
    spread = [dma((steps,)), dma((steps,)), dma((steps,)), dma((steps,)), dma((2 * steps,)), dma((2 * steps,))]
    ring = [dma((steps * PIECES,))] * 4 + [dma((n // 2 * PIECES,))] * 2
    outs = pl.pallas_call(
        functools.partial(kernel, n, pages),
        out_shape=(jax.ShapeDtypeStruct((TOK, QH * HD), jnp.bfloat16),
                   jax.ShapeDtypeStruct((ROWS, 2 * KV), jnp.bfloat16)),
        in_specs=[held, held, held, held, smem, smem],
        out_specs=(vmem, vmem),
        scratch_shapes=[
            pltpu.VMEM((TOK, QH * HD), jnp.bfloat16),
            pltpu.VMEM((TOK, 2 * KV), jnp.bfloat16),
            pltpu.VMEM((KERNEL, 2 * KV), jnp.float32),
            pltpu.VMEM((PIECES, KV, PIECE), jnp.bfloat16),
            pltpu.VMEM((2 * KVH, TOK, HD), jnp.float32),
            pltpu.VMEM((n, 8, KV), jnp.float32),
            pltpu.VMEM((n, PIECES, ROWS, PIECE), jnp.bfloat16),
            pltpu.VMEM((ROWS, 2 * KV), jnp.float32),
            pltpu.VMEM((QH * TOK, HD), jnp.bfloat16),
            pltpu.VMEM((QH * TOK, HD), jnp.float32),
            pltpu.VMEM((QH * TOK, HD), jnp.float32),
            pltpu.VMEM((pages, 2 * KV), jnp.float32),
            pltpu.VMEM((pages, 2 * KV), jnp.float32),
            pltpu.VMEM((CHUNK_BLOCKS * ROWS, 2 * KV), jnp.bfloat16),
            dma((PIECES + 3,)),
        ] + spread + ring,
        compiler_params=pltpu.CompilerParams(collective_id=0, has_side_effects=True),
    )(queries, keys_values, depth_kernel, point_weight, page_table, doc_lengths)
    return pl.pallas_call(
        place,
        out_shape=[jax.ShapeDtypeStruct(x.shape, x.dtype) for x in outs],
        in_specs=[vmem, vmem],
        out_specs=[hbm, hbm],
        scratch_shapes=[dma((2,))],
        compiler_params=pltpu.CompilerParams(vmem_limit_bytes=4 << 20),
    )(*outs)


def solution(mesh):
    placed = (P(("grp", "ctx"), None), P(("grp", "ctx"), None), P(), P(), P("grp"), P("grp"))
    return jax.shard_map(
        functools.partial(shards, mesh.shape["ctx"]),
        mesh=mesh,
        in_specs=placed,
        out_specs=(P(("grp", "ctx"), None), P(("grp", "ctx"), None)),
        check_vma=False,
    )
```
